256 devices in a mesh: pb: 16 (over y, x_hi, core), ga: 16 (over z, x_lo).
Axes of the slice: x: 4 (x_hi: 2, x_lo: 2; x = x_hi * 2 + x_lo), y: 4, z: 8, core: 2. Of those that a mesh axis runs over, the one named last changes fastest.
Arguments:
- elements: bfloat16 [16, 64, 112, 2048], P('pb', None, None, 'ga'), may hold values from -0.75 to 0.75
- screened: bfloat16 [16, 2048, 2048], P('pb', 'ga'), may hold values from -0.125 to 0.125
- counts: int32 [16], P('pb'), may hold values from 1536 to 2048
- k_minus_q: int32 [16], P('pb'), may hold values from 0 to 575
- occupation: float32 [576, 64], replicated, may hold values from 0.25 to 1
Outputs:
- sigma: float32 [112, 112], P('ga')
The draws below stay inside these ranges and needn't reach their ends.
Inputs may be any that keep to these rules, and one draw needn't show every extreme that they name: counts[q] G-vectors, the leading ones, lie inside the sphere of q. k_minus_q[q] is a row of occupation.
All inputs are finite; a program needn't handle non-finite values.
Results may differ from the reference program's by a relative error of at most 0.0029.
Values may be sent and summed in bfloat16 or wider, within the bound.
No kernel may reach another device: no remote copies, remote signals or barrier semaphores. Data moves between devices by JAX's collectives and lax.ppermute only.
A program may use at most 128 MiB of HBM per device.

```python
import jax
import jax.numpy as jnp
from jax import lax

G = 2048
S = 112
V = 64
NB = 32
KPTS = 576
Q = 16
N_GA = 16


def set_ends(drawn, own_key, smallest, largest):
    longest = drawn.shape.index(max(drawn.shape))
    spots = []
    for shift in (0, 1):
        where = [jax.random.randint(jax.random.fold_in(own_key, axis), (), 0, length) for axis, length in enumerate(drawn.shape)]
        where[longest] = (where[longest] + shift) % drawn.shape[longest]
        spots.append(tuple(where))
    return drawn.at[spots[0]].set(smallest).at[spots[1]].set(largest)


def levels(stream_key, dims, split, low, largest):
    factor_of = 1.0
    for axis_at, shards_of in split:
        steps = jax.random.uniform(jax.random.fold_in(jax.random.fold_in(stream_key, 6), axis_at), (shards_of,), jnp.float32, low / len(split), largest / len(split))
        factor_of = factor_of * jnp.repeat(jnp.exp(steps), dims[axis_at] // shards_of).reshape((-1,) + (1,) * (len(dims) - 1 - axis_at))
    return factor_of


def normal_values(own_key, dims, spread, bound, cuts=(), held_as=jnp.bfloat16):
    gain = levels(own_key, dims, cuts, -0.22, 0.18) if cuts else 1.0
    drawn = jax.random.normal(own_key, dims, jnp.float32) * spread * gain
    return jnp.minimum(jnp.maximum(drawn, -bound), bound).astype(held_as)


def setup_inputs(seed: int = 0) -> dict:
    key_of = jax.random.split(jax.random.key(seed), 6)
    elements = normal_values(key_of[0], (Q, V, S, G), (1.0 / (G * V) ** 0.25), 0.75, ((0, 16), (3, 16)))
    screened = normal_values(key_of[1], (Q, G, G), G ** -0.5, 0.125, ((0, 16), (1, 16)))
    counts = set_ends(jax.random.randint(key_of[2], (Q,), 3 * G // 4, G + 1), jax.random.fold_in(key_of[2], 1), 3 * G // 4, G).astype(jnp.int32)
    k_minus_q = set_ends(jax.random.randint(key_of[3], (Q,), 0, KPTS), jax.random.fold_in(key_of[3], 1), 0, KPTS - 1).astype(jnp.int32)
    occupation = jnp.clip(jax.random.uniform(key_of[4], (KPTS, V), jnp.float32, 0.25, 1.0), 0.25, 1.0)
    return {"elements": elements, "screened": screened, "counts": counts, "k_minus_q": k_minus_q, "occupation": occupation}


def reference(elements, screened, counts, k_minus_q, occupation):
    n_cycles = G // (N_GA * NB)
    g_index = jnp.arange(G, dtype=jnp.int32)
    k_index = jnp.arange(KPTS, dtype=jnp.int32)

    def single_q(inputs):
        element_q, stored_q, sphere_count, k_point = inputs
        w_true = stored_q.reshape(N_GA, n_cycles, NB, G).transpose(1, 0, 2, 3).reshape(G, G)
        inside = (g_index < sphere_count).astype(jnp.bfloat16)
        masked = element_q * inside[None, None, :]
        product = jnp.dot(masked.reshape(V * S, G), w_true, preferred_element_type=jnp.float32)
        product = product.astype(jnp.bfloat16).reshape(V, S, G)
        weights = jnp.sum(jnp.where((k_index == k_point)[:, None], occupation, jnp.float32(0.0)), axis=0)
        pair_terms = jnp.einsum("vmg,vng->vmn", product.astype(jnp.float32), masked.astype(jnp.float32), precision=lax.Precision.HIGHEST)
        return -jnp.einsum("v,vmn->mn", weights, pair_terms, precision=lax.Precision.HIGHEST)

    per_q = lax.map(single_q, (elements, screened, counts, k_minus_q))
    return jnp.sum(per_q, axis=0)
```

```python
import functools

import jax
import jax.numpy as jnp
from jax import lax
from jax.experimental import pallas as pl
from jax.experimental.pallas import tpu as pltpu
from jax.sharding import PartitionSpec as P

NB = 32
LANES = 128


def split_columns(scalars, stored, keep, send):
    me, count = scalars[0], scalars[1]
    x = lax.rem(me, 2)
    rows = stored.shape[0]
    row = lax.broadcasted_iota(jnp.int32, (rows, LANES), 0)
    lane = lax.broadcasted_iota(jnp.int32, (rows, LANES), 1)
    true_row = ((row // NB) * 16 + me) * NB + row % NB
    for s in range(keep.shape[1] // LANES):
        for out, parity in ((keep, x), (send, 1 - x)):
            first = pl.multiple_of((2 * s + parity) * LANES, LANES)
            inside = (true_row < count) & (lane + first < count)
            block = stored[:, pl.ds(first, LANES)].astype(jnp.float32)
            out[:, s * LANES : (s + 1) * LANES] = jnp.where(inside, block, 0.0).astype(out.dtype)


def contract(scalars, weights, own, other, w_keep, w_recv, sigma, w_sorted):
    x = lax.rem(scalars[0], 2)
    n_z, bands, states, _ = own.shape

    @pl.when(pl.program_id(0) == 0)
    def _():
        sigma[...] = jnp.zeros_like(sigma)
        for s in range(n_z):
            for slot in range(2):
                quarter = 2 * (s % 2) + (slot + x) % 2
                for u in range(2):
                    base = (2 * s + slot) * LANES + 2 * u * NB
                    w_sorted[pl.ds(pl.multiple_of(base + x * NB, NB), NB), :] = w_keep[2 * quarter + u, s // 2]
                    w_sorted[pl.ds(pl.multiple_of(base + (1 - x) * NB, NB), NB), :] = w_recv[2 * quarter + u, s // 2]

    lhs = jnp.concatenate(
        [part[s].reshape(bands * states, LANES) for s in range(n_z) for part in (own, other)], axis=1
    )
    product = jnp.dot(lhs, w_sorted[...], preferred_element_type=jnp.float32).astype(jnp.bfloat16)
    total = jnp.zeros((states, states), jnp.float32)
    for b in range(bands):
        right = jnp.concatenate([own[s, b] for s in range(n_z)], axis=1)
        pair = lax.dot_general(
            product[b * states : (b + 1) * states],
            right,
            (((1,), (1,)), ((), ())),
            preferred_element_type=jnp.float32,
        )
        total = total + weights[pl.program_id(0) * bands + b] * pair
    sigma[...] -= total


def on_device(elements, screened, counts, k_minus_q, occupation):
    _, n_band, n_state, g_slab = elements.shape
    groups = lax.axis_size("ga")
    n_z = groups // 2
    me = lax.axis_index("ga").astype(jnp.int32)
    z_groups = [[2 * z + x for z in range(n_z)] for x in range(2)]
    swap_x = [(i, i ^ 1) for i in range(groups)]
    scalars = jnp.stack([me, counts[0]])
    half = screened.shape[2] // 2

    keep, send = pl.pallas_call(
        split_columns,
        out_shape=[jax.ShapeDtypeStruct((g_slab, half), jnp.bfloat16)] * 2,
        in_specs=[pl.BlockSpec(memory_space=pltpu.SMEM), pl.BlockSpec(memory_space=pltpu.VMEM)],
        out_specs=[pl.BlockSpec(memory_space=pltpu.VMEM)] * 2,
    )(scalars, screened[0])
    recv = lax.ppermute(send, "ga", swap_x)
    w_keep = lax.all_gather(keep, "ga", axis_index_groups=z_groups)
    w_recv = lax.all_gather(recv, "ga", axis_index_groups=z_groups)

    own = lax.all_to_all(elements[0], "ga", 0, 0, axis_index_groups=z_groups, tiled=True)
    other = lax.ppermute(own, "ga", swap_x)
    bands = n_band // n_z
    own = own.reshape(n_z, bands, n_state, g_slab)
    other = other.reshape(n_z, bands, n_state, g_slab)
    w_keep = w_keep.reshape(n_z, g_slab // NB, NB, half)
    w_recv = w_recv.reshape(n_z, g_slab // NB, NB, half)
    weights = lax.dynamic_slice(occupation, (k_minus_q[0], (me // 2) * bands), (1, bands))[0]

    step = 2
    a_spec = pl.BlockSpec((n_z, step, n_state, g_slab), lambda i: (0, i, 0, 0))
    w_spec = pl.BlockSpec((n_z, g_slab // NB, NB, half), lambda i: (0, 0, 0, 0), pipeline_mode=pl.Buffered(1))
    partial_sum = pl.pallas_call(
        contract,
        grid=(bands // step,),
        out_shape=jax.ShapeDtypeStruct((n_state, n_state), jnp.float32),
        in_specs=[
            pl.BlockSpec(memory_space=pltpu.SMEM),
            pl.BlockSpec(memory_space=pltpu.SMEM),
            a_spec,
            a_spec,
            w_spec,
            w_spec,
        ],
        out_specs=pl.BlockSpec((n_state, n_state), lambda i: (0, 0)),
        scratch_shapes=[pltpu.VMEM((2 * half, half), jnp.bfloat16)],
        compiler_params=pltpu.CompilerParams(vmem_limit_bytes=48 * 1024 * 1024),
    )(scalars, weights, own, other, w_keep, w_recv)

    rows = n_state // groups
    shares = lax.all_to_all(partial_sum.reshape(groups, rows, n_state), "ga", 0, 0, tiled=True)
    share = jnp.sum(shares, axis=0)
    copies = jnp.broadcast_to(share[None], (lax.axis_size("pb"), rows, n_state))
    return jnp.sum(lax.all_to_all(copies, "pb", 0, 0, tiled=True), axis=0)


def solution(mesh):
    return jax.shard_map(
        on_device,
        mesh=mesh,
        in_specs=(P("pb", None, None, "ga"), P("pb", "ga", None), P("pb"), P("pb"), P()),
        out_specs=P("ga", None),
        check_vma=False,
    )
```

```python
import functools

import jax
import jax.numpy as jnp
from jax import lax
from jax.experimental import pallas as pl
from jax.experimental.pallas import tpu as pltpu
from jax.sharding import PartitionSpec as P

NB = 32
LANES = 128
SPACE = pltpu.VMEM


def prepare(bands, counts, k_minus_q, occupation, stored, keep, send, weights):
    me, count = lax.axis_index("ga"), counts[0]
    x = lax.rem(me, 2)
    rows = stored.shape[1]
    row = lax.broadcasted_iota(jnp.int32, (rows, LANES), 0)
    lane = lax.broadcasted_iota(jnp.int32, (rows, LANES), 1)
    true_row = ((row // NB) * 16 + me) * NB + row % NB
    for s in range(keep.shape[1] // LANES):
        for out, parity in ((keep, x), (send, 1 - x)):
            first = pl.multiple_of((2 * s + parity) * LANES, LANES)
            inside = (true_row < count) & (lane + first < count)
            block = stored[0, :, pl.ds(first, LANES)].astype(jnp.float32)
            out[:, s * LANES : (s + 1) * LANES] = jnp.where(inside, block, 0.0).astype(out.dtype)
    row_k = occupation[pl.ds(k_minus_q[0], 1), :]
    band = lax.broadcasted_iota(jnp.int32, row_k.shape, 1)
    for b in range(bands):
        weights[b] = jnp.sum(jnp.where(band == (me // 2) * bands + b, row_k, 0.0))


def contract(n_z, weights, *refs):
    own, other = refs[:n_z], refs[n_z : 2 * n_z]
    rings = refs[2 * n_z : 3 * n_z], refs[3 * n_z : 4 * n_z]
    sigma, a_sorted, w_sorted = refs[4 * n_z :]
    me = lax.axis_index("ga")
    x, z = lax.rem(me, 2), me // 2
    bands, states, rows = own[0].shape

    for k in range(n_z):
        source = lax.rem(z + n_z - k, n_z)
        a_sorted[2 * source + x] = own[k][...]
        a_sorted[2 * source + 1 - x] = other[k][...]
        for ring, x_of in zip(rings, (x, 1 - x)):
            for c in range(rows // NB):
                to = (4 * c + source // 2) * LANES + (2 * lax.rem(source, 2) + x_of) * NB
                w_sorted[pl.ds(pl.multiple_of(to, NB), NB), :] = ring[k][c * NB : (c + 1) * NB, :]

    step = 2

    def some_bands(at, total):
        b = at * step
        lhs = jnp.concatenate(
            [a_sorted[i, pl.ds(b, step)].reshape(step * states, LANES) for i in range(2 * n_z)], axis=1
        )
        product = jnp.dot(lhs, w_sorted[...], preferred_element_type=jnp.float32).astype(jnp.bfloat16)
        for j in range(step):
            right = jnp.concatenate([a_sorted[2 * s + x, b + j] for s in range(n_z)], axis=1)
            pair = lax.dot_general(
                product[j * states : (j + 1) * states],
                right,
                (((1,), (1,)), ((), ())),
                preferred_element_type=jnp.float32,
            )
            total = total - weights[b + j] * pair
        return total

    sigma[...] = lax.fori_loop(0, bands // step, some_bands, jnp.zeros((states, states), jnp.float32))


def on_device(elements, screened, counts, k_minus_q, occupation):
    _, n_band, n_state, g_slab = elements.shape
    groups = lax.axis_size("ga")
    n_z = groups // 2
    z = lax.axis_index("ga") // 2
    bands = n_band // n_z
    half_columns = screened.shape[2] // 2

    def over_x(value):
        return lax.ppermute(value, "ga", [(i, i ^ 1) for i in range(groups)])

    def over_z(value, k):
        return lax.ppermute(value, "ga", [(i, (i + 2 * k) % groups) for i in range(groups)])

    keep, send, weights = pl.pallas_call(
        functools.partial(prepare, bands),
        out_shape=[jax.ShapeDtypeStruct((g_slab, half_columns), jnp.bfloat16)] * 2
        + [jax.ShapeDtypeStruct((bands,), jnp.float32)],
        in_specs=[pl.BlockSpec(memory_space=pltpu.SMEM)] * 2 + [pl.BlockSpec(memory_space=pltpu.VMEM)] * 2,
        out_specs=[pl.BlockSpec(memory_space=pltpu.VMEM)] * 2 + [pl.BlockSpec(memory_space=pltpu.SMEM)],
    )(counts, k_minus_q, occupation, screened)

    slabs = elements[0].reshape(n_z, bands, n_state, g_slab)
    own, other = [None] * n_z, [None] * n_z
    for k in range(n_z):
        own[k] = lax.dynamic_index_in_dim(slabs, (z + k) % n_z, 0, keepdims=False)
    for k in range(1, n_z):
        own[k] = over_z(own[k], k)
    recv = over_x(send)
    tie = lax.optimization_barrier
    ring_k, ring_r = [keep] + [None] * (n_z - 1), [recv] + [None] * (n_z - 1)
    ring_k[0], own[1], own[7] = tie((ring_k[0], own[1], own[7]))
    ring_k[1], ring_k[7] = over_z(ring_k[0], 1), over_z(ring_k[0], -1)
    ring_r[1], ring_r[7] = over_z(ring_r[0], 1), over_z(ring_r[0], -1)
    ring_k[1], ring_k[7], own[2], own[6] = tie((ring_k[1], ring_k[7], own[2], own[6]))
    ring_k[2], ring_k[6] = over_z(ring_k[1], 1), over_z(ring_k[7], -1)
    ring_r[2], ring_r[6] = over_z(ring_r[1], 1), over_z(ring_r[7], -1)
    ring_k[2], ring_k[6], own[3], own[5] = tie((ring_k[2], ring_k[6], own[3], own[5]))
    ring_k[3], ring_k[5] = over_z(ring_k[2], 1), over_z(ring_k[6], -1)
    ring_r[3], ring_r[5] = over_z(ring_r[2], 1), over_z(ring_r[6], -1)
    ring_k[3], own[4] = tie((ring_k[3], own[4]))
    ring_k[4], ring_r[4] = over_z(ring_k[3], 1), over_z(ring_r[5], -1)
    for k in range(n_z):
        other[k] = over_x(own[k])

    operands = [pltpu.with_memory_space_constraint(v, SPACE) for v in own + other + ring_k + ring_r]
    partial_sum = pl.pallas_call(
        functools.partial(contract, n_z),
        out_shape=jax.ShapeDtypeStruct((n_state, n_state), jnp.float32),
        in_specs=[pl.BlockSpec(memory_space=pltpu.SMEM)] + [pl.BlockSpec(memory_space=pltpu.VMEM)] * (4 * n_z),
        out_specs=pl.BlockSpec(memory_space=pltpu.VMEM),
        scratch_shapes=[
            pltpu.VMEM((groups, bands, n_state, g_slab), jnp.bfloat16),
            pltpu.VMEM((2 * half_columns, half_columns), jnp.bfloat16),
        ],
        compiler_params=pltpu.CompilerParams(vmem_limit_bytes=24 * 1024 * 1024),
    )(weights, *operands)

    rows = n_state // groups
    shares = lax.all_to_all(partial_sum.reshape(groups, rows, n_state), "ga", 0, 0, tiled=True)
    share = jnp.sum(shares, axis=0)
    copies = jnp.broadcast_to(share[None], (lax.axis_size("pb"), rows, n_state))
    return jnp.sum(lax.all_to_all(copies, "pb", 0, 0, tiled=True), axis=0)


def solution(mesh):
    return jax.shard_map(
        on_device,
        mesh=mesh,
        in_specs=(P("pb", None, None, "ga"), P("pb", "ga", None), P("pb"), P("pb"), P()),
        out_specs=P("ga", None),
        check_vma=False,
    )
```

```python
import functools

import jax
import jax.numpy as jnp
from jax import lax
from jax.experimental import pallas as pl
from jax.experimental.pallas import tpu as pltpu
from jax.sharding import PartitionSpec as P

NB = 32
LANES = 128
VMEM = pl.BlockSpec(memory_space=pltpu.VMEM)
SMEM = pl.BlockSpec(memory_space=pltpu.SMEM)
STEP = 2


def position():
    me = lax.axis_index("ga")
    return me, lax.rem(me, 2), me // 2


def prepare(counts, k_minus_q, occupation, stored, keep, send, weights):
    me, x, z = position()
    count = counts[0]
    bands = weights.shape[0]
    rows = stored.shape[1]
    row = lax.broadcasted_iota(jnp.int32, (rows, LANES), 0)
    lane = lax.broadcasted_iota(jnp.int32, (rows, LANES), 1)
    true_row = ((row // NB) * 16 + me) * NB + row % NB
    for s in range(keep.shape[1] // LANES):
        for out, parity in ((keep, x), (send, 1 - x)):
            first = pl.multiple_of((2 * s + parity) * LANES, LANES)
            inside = (true_row < count) & (lane + first < count)
            block = stored[0, :, pl.ds(first, LANES)].astype(jnp.float32)
            out[:, s * LANES : (s + 1) * LANES] = jnp.where(inside, block, 0.0).astype(out.dtype)
    mine = occupation[pl.ds(pl.multiple_of(z * bands, bands), bands), :]
    k_point = lax.broadcasted_iota(jnp.int32, mine.shape, 1)
    mine = jnp.where(k_point == k_minus_q[0], mine, 0.0)
    for b in range(bands):
        weights[b] = jnp.sum(mine[b : b + 1])


def row_of(source, c, x_of):
    return (4 * c + source // 2) * LANES + (2 * lax.rem(source, 2) + x_of) * NB


def contract_most(n_z, *refs):
    own, other = refs[:2]
    rings = refs[2 : n_z + 1], refs[n_z + 1 : 2 * n_z]
    a_sorted, product, w_sorted = refs[2 * n_z :]
    _, x, z = position()
    _, bands, states, rows = a_sorted.shape
    half = n_z // 2

    for k in range(n_z):
        source = lax.rem(z + n_z - k, n_z)
        a_sorted[2 * source + x] = own[k * bands : (k + 1) * bands]
        a_sorted[2 * source + 1 - x] = other[k * bands : (k + 1) * bands]
        for ring, x_of in zip(rings, (x, 1 - x)):
            for c in range(rows // NB):
                to = pl.ds(pl.multiple_of(row_of(source, c, x_of), NB), NB)
                if k == half:
                    w_sorted[to, :] = jnp.zeros((NB, w_sorted.shape[1]), w_sorted.dtype)
                else:
                    w_sorted[to, :] = ring[k - (k > half)][c * NB : (c + 1) * NB, :]

    def some_bands(at, carry):
        b = at * STEP
        lhs = jnp.concatenate(
            [a_sorted[i, pl.ds(b, STEP)].reshape(STEP * states, LANES) for i in range(2 * n_z)], axis=1
        )
        product[at] = jnp.dot(lhs, w_sorted[...], preferred_element_type=jnp.float32)
        return carry

    lax.fori_loop(0, bands // STEP, some_bands, 0)


def contract_rest(n_z, weights, a_sorted, product, far_keep, far_recv, sigma, w_far):
    _, x, z = position()
    _, bands, states, rows = a_sorted.shape
    source = lax.rem(z + n_z // 2, n_z)
    cycles = rows // NB
    w_far[...] = jnp.zeros_like(w_far)
    for ref, x_of in ((far_keep, x), (far_recv, 1 - x)):
        for c in range(cycles):
            to = c * LANES + (2 * lax.rem(source, 2) + x_of) * NB
            w_far[pl.ds(pl.multiple_of(to, NB), NB), :] = ref[c * NB : (c + 1) * NB, :]

    def some_bands(at, total):
        b = at * STEP
        lhs = jnp.concatenate(
            [a_sorted[4 * c + source // 2, pl.ds(b, STEP)].reshape(STEP * states, LANES) for c in range(cycles)], axis=1
        )
        whole = product[at] + jnp.dot(lhs, w_far[...], preferred_element_type=jnp.float32)
        whole = whole.astype(jnp.bfloat16)
        for j in range(STEP):
            right = jnp.concatenate([a_sorted[2 * s + x, b + j] for s in range(n_z)], axis=1)
            pair = lax.dot_general(
                whole[j * states : (j + 1) * states],
                right,
                (((1,), (1,)), ((), ())),
                preferred_element_type=jnp.float32,
            )
            total = total - weights[b + j] * pair
        return total

    total = lax.fori_loop(0, bands // STEP, some_bands, jnp.zeros((states, states), jnp.float32))
    share = sigma.shape[1]
    for i in range(sigma.shape[0]):
        sigma[i] = total[i * share : (i + 1) * share]


def in_vmem(values):
    return [pltpu.with_memory_space_constraint(v, pltpu.VMEM) for v in values]


def pack(*refs):
    first = 0
    for ref in refs[:-1]:
        refs[-1][first : first + ref.shape[0]] = ref[...]
        first += ref.shape[0]


def packed(pieces):
    total = sum(piece.shape[0] for piece in pieces)
    return pl.pallas_call(
        pack,
        out_shape=jax.ShapeDtypeStruct((total, *pieces[0].shape[1:]), pieces[0].dtype),
        in_specs=[VMEM] * len(pieces),
        out_specs=VMEM,
    )(*in_vmem(pieces))


def on_device(elements, screened, counts, k_minus_q, occupation):
    _, n_band, n_state, g_slab = elements.shape
    groups = lax.axis_size("ga")
    n_z = groups // 2
    bands = n_band // n_z
    half_columns = screened.shape[2] // 2
    slab_shape = jax.ShapeDtypeStruct((bands, n_state, g_slab), jnp.bfloat16)
    half_shape = jax.ShapeDtypeStruct((g_slab, half_columns), jnp.bfloat16)
    limit = pltpu.CompilerParams(vmem_limit_bytes=20 * 1024 * 1024)

    def over_x(value):
        return lax.ppermute(value, "ga", [(i, i ^ 1) for i in range(groups)])

    def over_z(value, k):
        return lax.ppermute(value, "ga", [(i, (i + 2 * k) % groups) for i in range(groups)])

    keep, send, weights = pl.pallas_call(
        prepare,
        out_shape=[half_shape] * 2 + [jax.ShapeDtypeStruct((bands,), jnp.float32)],
        in_specs=[SMEM] * 2 + [VMEM] * 2,
        out_specs=[VMEM] * 2 + [SMEM],
    )(counts, k_minus_q, occupation.T, screened)

    slabs = elements[0].reshape(n_z, bands, n_state, g_slab)
    z = lax.axis_index("ga") // 2
    own = [lax.dynamic_index_in_dim(slabs, (z + k) % n_z, 0, keepdims=False) for k in range(n_z)]
    tie = lax.optimization_barrier
    opposite = [own[4][: bands // 2], own[4][bands // 2 :]]
    opposite = [over_z(opposite[0], 2), over_z(opposite[1], -2)]
    for k in (1, 7, 2, 6, 3, 5):
        own[k] = over_z(own[k], k)
    opposite = [over_z(opposite[0], 2), over_z(opposite[1], -2)]
    recv = over_x(send)
    ring_k, ring_r = [keep] + [None] * (n_z - 1), [recv] + [None] * (n_z - 1)
    own[1], own[7], own[2], own[6], own[3], own[5], opposite[0], opposite[1], ring_k[0], ring_r[0] = tie(
        (own[1], own[7], own[2], own[6], own[3], own[5], opposite[0], opposite[1], ring_k[0], ring_r[0])
    )
    own_all = packed(own[:4] + opposite + own[5:])
    other_all = over_x(own_all)
    ring_k[1], ring_k[7] = over_z(ring_k[0], 1), over_z(ring_k[0], -1)
    ring_r[1], ring_r[7] = over_z(ring_r[0], 1), over_z(ring_r[0], -1)
    ring_k[1], ring_k[7] = tie((ring_k[1], ring_k[7]))
    ring_r[1], ring_r[7] = tie((ring_r[1], ring_r[7]))
    ring_k[2], ring_k[6] = over_z(ring_k[1], 1), over_z(ring_k[7], -1)
    ring_r[2], ring_r[6] = over_z(ring_r[1], 1), over_z(ring_r[7], -1)
    ring_k[2], ring_k[6] = tie((ring_k[2], ring_k[6]))
    ring_r[2], ring_r[6] = tie((ring_r[2], ring_r[6]))
    ring_k[3], ring_k[5] = over_z(ring_k[2], 1), over_z(ring_k[6], -1)
    ring_r[3], ring_r[5] = over_z(ring_r[2], 1), over_z(ring_r[6], -1)
    ring_k[3], ring_k[5] = tie((ring_k[3], ring_k[5]))
    ring_r[3], ring_r[5], other_all = tie((ring_r[3], ring_r[5], other_all))
    ring_k[4], ring_r[4] = over_z(ring_k[3], 1), over_z(ring_r[5], -1)

    a_sorted, product = pl.pallas_call(
        functools.partial(contract_most, n_z),
        out_shape=[
            jax.ShapeDtypeStruct((groups, *slab_shape.shape), jnp.bfloat16),
            jax.ShapeDtypeStruct((bands // STEP, STEP * n_state, half_columns), jnp.float32),
        ],
        in_specs=[VMEM] * (2 * n_z),
        out_specs=[VMEM] * 2,
        scratch_shapes=[pltpu.VMEM((2 * half_columns, half_columns), jnp.bfloat16)],
        compiler_params=limit,
    )(*in_vmem([own_all, other_all] + ring_k[:4] + ring_k[5:] + ring_r[:4] + ring_r[5:]))
    shares = pl.pallas_call(
        functools.partial(contract_rest, n_z),
        out_shape=jax.ShapeDtypeStruct((groups, n_state // groups, n_state), jnp.float32),
        in_specs=[SMEM] + [VMEM] * 4,
        out_specs=VMEM,
        scratch_shapes=[pltpu.VMEM((half_columns // 2, half_columns), jnp.bfloat16)],
        compiler_params=limit,
    )(weights, *in_vmem([a_sorted, product, ring_k[4], ring_r[4]]))

    share = jnp.sum(lax.all_to_all(shares, "ga", 0, 0, tiled=True), axis=0)
    copies = jnp.broadcast_to(share[None], (lax.axis_size("pb"), *share.shape))
    return jnp.sum(lax.all_to_all(copies, "pb", 0, 0, tiled=True), axis=0)


def solution(mesh):
    return jax.shard_map(
        on_device,
        mesh=mesh,
        in_specs=(P("pb", None, None, "ga"), P("pb", "ga", None), P("pb"), P("pb"), P()),
        out_specs=P("ga", None),
        check_vma=False,
    )
```

```python
import functools

import jax
import jax.numpy as jnp
from jax import lax
from jax.experimental import pallas as pl
from jax.experimental.pallas import tpu as pltpu
from jax.sharding import PartitionSpec as P

NB = 32
LANES = 128
VMEM = pl.BlockSpec(memory_space=pltpu.VMEM)
SMEM = pl.BlockSpec(memory_space=pltpu.SMEM)
STEP = 2


def position():
    me = lax.axis_index("ga")
    return me, lax.rem(me, 2), me // 2


def prepare(counts, k_minus_q, occupation, stored, keep, send, weights):
    me, x, z = position()
    count = counts[0]
    bands = weights.shape[0]
    rows = stored.shape[1]
    row = lax.broadcasted_iota(jnp.int32, (rows, LANES), 0)
    lane = lax.broadcasted_iota(jnp.int32, (rows, LANES), 1)
    true_row = ((row // NB) * 16 + me) * NB + row % NB
    for s in range(keep.shape[1] // LANES):
        for out, parity in ((keep, x), (send, 1 - x)):
            first = pl.multiple_of((2 * s + parity) * LANES, LANES)
            inside = (true_row < count) & (lane + first < count)
            block = stored[0, :, pl.ds(first, LANES)].astype(jnp.float32)
            out[:, s * LANES : (s + 1) * LANES] = jnp.where(inside, block, 0.0).astype(out.dtype)
    mine = occupation[pl.ds(pl.multiple_of(z * bands, bands), bands), :]
    k_point = lax.broadcasted_iota(jnp.int32, mine.shape, 1)
    mine = jnp.where(k_point == k_minus_q[0], mine, 0.0)
    for b in range(bands):
        weights[b] = jnp.sum(mine[b : b + 1])


def row_of(source, c, x_of):
    return (4 * c + source // 2) * LANES + (2 * lax.rem(source, 2) + x_of) * NB


def contract_most(n_z, *refs):
    own, other = refs[:2]
    rings = refs[2 : n_z + 1], refs[n_z + 1 : 2 * n_z]
    a_sorted, product, w_sorted = refs[2 * n_z :]
    _, x, z = position()
    _, bands, states, rows = a_sorted.shape
    half = n_z // 2

    for k in range(n_z):
        source = lax.rem(z + n_z - k, n_z)
        a_sorted[2 * source + x] = own[k * bands : (k + 1) * bands]
        a_sorted[2 * source + 1 - x] = other[k * bands : (k + 1) * bands]
        for ring, x_of in zip(rings, (x, 1 - x)):
            for c in range(rows // NB):
                to = pl.ds(pl.multiple_of(row_of(source, c, x_of), NB), NB)
                if k == half:
                    w_sorted[to, :] = jnp.zeros((NB, w_sorted.shape[1]), w_sorted.dtype)
                else:
                    w_sorted[to, :] = ring[k - (k > half)][c * NB : (c + 1) * NB, :]

    def some_bands(at, carry):
        b = at * STEP
        lhs = jnp.concatenate(
            [a_sorted[i, pl.ds(b, STEP)].reshape(STEP * states, LANES) for i in range(2 * n_z)], axis=1
        )
        product[at] = jnp.dot(lhs, w_sorted[...], preferred_element_type=jnp.float32)
        return carry

    lax.fori_loop(0, bands // STEP, some_bands, 0)


def contract_rest(n_z, weights, a_sorted, product, far_keep, far_recv, sigma, w_far):
    _, x, z = position()
    _, bands, states, rows = a_sorted.shape
    source = lax.rem(z + n_z // 2, n_z)
    cycles = rows // NB
    w_far[...] = jnp.zeros_like(w_far)
    for ref, x_of in ((far_keep, x), (far_recv, 1 - x)):
        for c in range(cycles):
            to = c * LANES + (2 * lax.rem(source, 2) + x_of) * NB
            w_far[pl.ds(pl.multiple_of(to, NB), NB), :] = ref[c * NB : (c + 1) * NB, :]

    def some_bands(at, total):
        b = at * STEP
        lhs = jnp.concatenate(
            [a_sorted[4 * c + source // 2, pl.ds(b, STEP)].reshape(STEP * states, LANES) for c in range(cycles)], axis=1
        )
        whole = product[at] + jnp.dot(lhs, w_far[...], preferred_element_type=jnp.float32)
        whole = whole.astype(jnp.bfloat16)
        for j in range(STEP):
            right = jnp.concatenate([a_sorted[2 * s + x, b + j] for s in range(n_z)], axis=1)
            pair = lax.dot_general(
                whole[j * states : (j + 1) * states],
                right,
                (((1,), (1,)), ((), ())),
                preferred_element_type=jnp.float32,
            )
            total = total - weights[b + j] * pair
        return total

    total = lax.fori_loop(0, bands // STEP, some_bands, jnp.zeros((states, states), jnp.float32))
    share = sigma.shape[1]
    for i in range(sigma.shape[0]):
        sigma[i] = total[i * share : (i + 1) * share]


def in_vmem(values):
    return [pltpu.with_memory_space_constraint(v, pltpu.VMEM) for v in values]


def pack(*refs):
    first = 0
    for ref in refs[:-1]:
        refs[-1][first : first + ref.shape[0]] = ref[...]
        first += ref.shape[0]


def packed(pieces):
    total = sum(piece.shape[0] for piece in pieces)
    return pl.pallas_call(
        pack,
        out_shape=pltpu.VMEM((total, *pieces[0].shape[1:]), pieces[0].dtype),
        in_specs=[VMEM] * len(pieces),
        out_specs=VMEM,
        compiler_params=pltpu.CompilerParams(vmem_limit_bytes=4 * 1024 * 1024),
    )(*in_vmem(pieces))


def on_device(elements, screened, counts, k_minus_q, occupation):
    _, n_band, n_state, g_slab = elements.shape
    groups = lax.axis_size("ga")
    n_z = groups // 2
    bands = n_band // n_z
    half_columns = screened.shape[2] // 2
    slab_shape = jax.ShapeDtypeStruct((bands, n_state, g_slab), jnp.bfloat16)
    half_shape = jax.ShapeDtypeStruct((g_slab, half_columns), jnp.bfloat16)
    limit = pltpu.CompilerParams(vmem_limit_bytes=20 * 1024 * 1024)

    def over_x(value):
        return lax.ppermute(value, "ga", [(i, i ^ 1) for i in range(groups)])

    def over_z(value, k):
        return lax.ppermute(value, "ga", [(i, (i + 2 * k) % groups) for i in range(groups)])

    keep, send, weights = pl.pallas_call(
        prepare,
        out_shape=[half_shape] * 2 + [jax.ShapeDtypeStruct((bands,), jnp.float32)],
        in_specs=[SMEM] * 2 + [VMEM] * 2,
        out_specs=[VMEM] * 2 + [SMEM],
        compiler_params=pltpu.CompilerParams(vmem_limit_bytes=4 * 1024 * 1024),
    )(counts, k_minus_q, occupation.T, screened)

    slabs = elements[0].reshape(n_z, bands, n_state, g_slab)
    z = lax.axis_index("ga") // 2
    own = [lax.dynamic_index_in_dim(slabs, (z + k) % n_z, 0, keepdims=False) for k in range(n_z)]
    tie = lax.optimization_barrier
    opposite = [own[4][: bands // 2], own[4][bands // 2 :]]
    opposite = [over_z(opposite[0], 2), over_z(opposite[1], -2)]
    for k in (1, 7, 2, 6, 3, 5):
        own[k] = over_z(own[k], k)
    opposite = [over_z(opposite[0], 2), over_z(opposite[1], -2)]
    recv = over_x(send)
    ring_k, ring_r = [keep] + [None] * (n_z - 1), [recv] + [None] * (n_z - 1)
    own[1], own[7], own[2], own[6], own[3], own[5], opposite[0], opposite[1], ring_k[0], ring_r[0] = tie(
        (own[1], own[7], own[2], own[6], own[3], own[5], opposite[0], opposite[1], ring_k[0], ring_r[0])
    )
    own_all = packed(own[:4] + opposite + own[5:])
    other_all = over_x(own_all)
    ring_k[1], ring_k[7] = over_z(ring_k[0], 1), over_z(ring_k[0], -1)
    ring_r[1], ring_r[7] = over_z(ring_r[0], 1), over_z(ring_r[0], -1)
    ring_k[1], ring_k[7] = tie((ring_k[1], ring_k[7]))
    ring_r[1], ring_r[7] = tie((ring_r[1], ring_r[7]))
    ring_k[2], ring_k[6] = over_z(ring_k[1], 1), over_z(ring_k[7], -1)
    ring_r[2], ring_r[6] = over_z(ring_r[1], 1), over_z(ring_r[7], -1)
    ring_k[2], ring_k[6] = tie((ring_k[2], ring_k[6]))
    ring_r[2], ring_r[6] = tie((ring_r[2], ring_r[6]))
    ring_k[3], ring_k[5] = over_z(ring_k[2], 1), over_z(ring_k[6], -1)
    ring_r[3], ring_r[5] = over_z(ring_r[2], 1), over_z(ring_r[6], -1)
    ring_k[3], ring_k[5] = tie((ring_k[3], ring_k[5]))
    ring_r[3], ring_r[5], other_all = tie((ring_r[3], ring_r[5], other_all))
    ring_k[4], ring_r[4] = over_z(ring_k[3], 1), over_z(ring_r[5], -1)

    a_sorted, product = pl.pallas_call(
        functools.partial(contract_most, n_z),
        out_shape=[
            jax.ShapeDtypeStruct((groups, *slab_shape.shape), jnp.bfloat16),
            jax.ShapeDtypeStruct((bands // STEP, STEP * n_state, half_columns), jnp.float32),
        ],
        in_specs=[VMEM] * (2 * n_z),
        out_specs=[VMEM] * 2,
        scratch_shapes=[pltpu.VMEM((2 * half_columns, half_columns), jnp.bfloat16)],
        compiler_params=limit,
    )(*in_vmem([own_all, other_all] + ring_k[:4] + ring_k[5:] + ring_r[:4] + ring_r[5:]))
    shares = pl.pallas_call(
        functools.partial(contract_rest, n_z),
        out_shape=jax.ShapeDtypeStruct((groups, n_state // groups, n_state), jnp.float32),
        in_specs=[SMEM] + [VMEM] * 4,
        out_specs=VMEM,
        scratch_shapes=[pltpu.VMEM((half_columns // 2, half_columns), jnp.bfloat16)],
        compiler_params=limit,
    )(weights, *in_vmem([a_sorted, product, ring_k[4], ring_r[4]]))

    layers = [[2 * z_at + x_at for x_at in range(2)] for z_at in range(n_z)]
    by_z = [[2 * z_at + x_at for z_at in range(n_z)] for x_at in range(2)]
    shares = shares.reshape(n_z, 2, *shares.shape[1:])
    share = jnp.sum(lax.all_to_all(shares, "ga", 0, 0, axis_index_groups=by_z, tiled=True), axis=0)
    n_pb = lax.axis_size("pb")
    copies = jnp.broadcast_to(share[None], (n_pb, *share.shape)).reshape(n_pb * 2, *share.shape[1:])
    planes = [[p * groups + i for p in range(n_pb) for i in layer] for layer in layers]
    received = lax.all_to_all(copies, ("pb", "ga"), 0, 0, axis_index_groups=planes, tiled=True)
    return jnp.sum(received, axis=0)


def solution(mesh):
    return jax.shard_map(
        on_device,
        mesh=mesh,
        in_specs=(P("pb", None, None, "ga"), P("pb", "ga", None), P("pb"), P("pb"), P()),
        out_specs=P("ga", None),
        check_vma=False,
    )
```

```python
import functools

import jax
import jax.numpy as jnp
from jax import lax
from jax.experimental import pallas as pl
from jax.experimental.pallas import tpu as pltpu
from jax.sharding import PartitionSpec as P

NB = 32
LANES = 128
VMEM = pl.BlockSpec(memory_space=pltpu.VMEM)
SMEM = pl.BlockSpec(memory_space=pltpu.SMEM)
STEP = 8


def position():
    me = lax.axis_index("ga")
    return me, lax.rem(me, 2), me // 2


def prepare(counts, k_minus_q, occupation, stored, keep, send, weights):
    me, x, z = position()
    count = counts[0]
    bands = weights.shape[0]
    rows = stored.shape[1]
    row = lax.broadcasted_iota(jnp.int32, (rows, LANES), 0)
    lane = lax.broadcasted_iota(jnp.int32, (rows, LANES), 1)
    true_row = ((row // NB) * 16 + me) * NB + row % NB
    for s in range(keep.shape[1] // LANES):
        for out, parity in ((keep, x), (send, 1 - x)):
            first = pl.multiple_of((2 * s + parity) * LANES, LANES)
            inside = (true_row < count) & (lane + first < count)
            block = stored[0, :, pl.ds(first, LANES)].astype(jnp.float32)
            out[:, s * LANES : (s + 1) * LANES] = jnp.where(inside, block, 0.0).astype(out.dtype)
    mine = occupation[pl.ds(pl.multiple_of(z * bands, bands), bands), :]
    k_point = lax.broadcasted_iota(jnp.int32, mine.shape, 1)
    mine = jnp.where(k_point == k_minus_q[0], mine, 0.0)
    for b in range(bands):
        weights[b] = jnp.sum(mine[b : b + 1])


def row_of(source, c, x_of):
    return (4 * c + source // 2) * LANES + (2 * lax.rem(source, 2) + x_of) * NB


def contract_most(n_z, *refs):
    own, other = refs[:2]
    rings = refs[2 : n_z + 1], refs[n_z + 1 : 2 * n_z]
    a_sorted, product, w_sorted = refs[2 * n_z :]
    _, x, z = position()
    _, bands, states, rows = a_sorted.shape
    half = n_z // 2

    for k in range(n_z):
        source = lax.rem(z + n_z - k, n_z)
        a_sorted[2 * source + x] = own[k * bands : (k + 1) * bands]
        a_sorted[2 * source + 1 - x] = other[k * bands : (k + 1) * bands]
        for ring, x_of in zip(rings, (x, 1 - x)):
            for c in range(rows // NB):
                to = pl.ds(pl.multiple_of(row_of(source, c, x_of), NB), NB)
                if k == half:
                    w_sorted[to, :] = jnp.zeros((NB, w_sorted.shape[1]), w_sorted.dtype)
                else:
                    w_sorted[to, :] = ring[k - (k > half)][c * NB : (c + 1) * NB, :]

    def some_bands(at, carry):
        b = at * STEP
        lhs = jnp.concatenate(
            [a_sorted[i, pl.ds(b, STEP)].reshape(STEP * states, LANES) for i in range(2 * n_z)], axis=1
        )
        product[at] = jnp.dot(lhs, w_sorted[...], preferred_element_type=jnp.float32)
        return carry

    lax.fori_loop(0, bands // STEP, some_bands, 0)


def contract_rest(n_z, weights, a_sorted, product, far_keep, far_recv, sigma, w_far):
    _, x, z = position()
    _, bands, states, rows = a_sorted.shape
    source = lax.rem(z + n_z // 2, n_z)
    cycles = rows // NB
    w_far[...] = jnp.zeros_like(w_far)
    for ref, x_of in ((far_keep, x), (far_recv, 1 - x)):
        for c in range(cycles):
            to = c * LANES + (2 * lax.rem(source, 2) + x_of) * NB
            w_far[pl.ds(pl.multiple_of(to, NB), NB), :] = ref[c * NB : (c + 1) * NB, :]

    def some_bands(at, total):
        b = at * STEP
        lhs = jnp.concatenate(
            [a_sorted[4 * c + source // 2, pl.ds(b, STEP)].reshape(STEP * states, LANES) for c in range(cycles)], axis=1
        )
        whole = product[at] + jnp.dot(lhs, w_far[...], preferred_element_type=jnp.float32)
        whole = whole.astype(jnp.bfloat16)
        for j in range(STEP):
            right = jnp.concatenate([a_sorted[2 * s + x, b + j] for s in range(n_z)], axis=1)
            pair = lax.dot_general(
                whole[j * states : (j + 1) * states],
                right,
                (((1,), (1,)), ((), ())),
                preferred_element_type=jnp.float32,
            )
            total = total - weights[b + j] * pair
        return total

    total = lax.fori_loop(0, bands // STEP, some_bands, jnp.zeros((states, states), jnp.float32))
    share = sigma.shape[1]
    for i in range(sigma.shape[0]):
        sigma[i] = total[i * share : (i + 1) * share]


def in_vmem(values):
    return [pltpu.with_memory_space_constraint(v, pltpu.VMEM) for v in values]


def pack(*refs):
    first = 0
    for ref in refs[:-1]:
        refs[-1][first : first + ref.shape[0]] = ref[...]
        first += ref.shape[0]


def packed(pieces):
    total = sum(piece.shape[0] for piece in pieces)
    return pl.pallas_call(
        pack,
        out_shape=pltpu.VMEM((total, *pieces[0].shape[1:]), pieces[0].dtype),
        in_specs=[VMEM] * len(pieces),
        out_specs=VMEM,
        compiler_params=pltpu.CompilerParams(vmem_limit_bytes=4 * 1024 * 1024),
    )(*in_vmem(pieces))


def on_device(elements, screened, counts, k_minus_q, occupation):
    _, n_band, n_state, g_slab = elements.shape
    groups = lax.axis_size("ga")
    n_z = groups // 2
    bands = n_band // n_z
    half_columns = screened.shape[2] // 2
    slab_shape = jax.ShapeDtypeStruct((bands, n_state, g_slab), jnp.bfloat16)
    half_shape = jax.ShapeDtypeStruct((g_slab, half_columns), jnp.bfloat16)
    limit = pltpu.CompilerParams(vmem_limit_bytes=20 * 1024 * 1024)

    def over_x(value):
        return lax.ppermute(value, "ga", [(i, i ^ 1) for i in range(groups)])

    def over_z(value, k):
        return lax.ppermute(value, "ga", [(i, (i + 2 * k) % groups) for i in range(groups)])

    keep, send, weights = pl.pallas_call(
        prepare,
        out_shape=[half_shape] * 2 + [jax.ShapeDtypeStruct((bands,), jnp.float32)],
        in_specs=[SMEM] * 2 + [VMEM] * 2,
        out_specs=[VMEM] * 2 + [SMEM],
        compiler_params=pltpu.CompilerParams(vmem_limit_bytes=4 * 1024 * 1024),
    )(counts, k_minus_q, occupation.T, screened)

    slabs = elements[0].reshape(n_z, bands, n_state, g_slab)
    z = lax.axis_index("ga") // 2
    own = [lax.dynamic_index_in_dim(slabs, (z + k) % n_z, 0, keepdims=False) for k in range(n_z)]
    tie = lax.optimization_barrier
    opposite = [own[4][: bands // 2], own[4][bands // 2 :]]
    opposite = [over_z(opposite[0], 2), over_z(opposite[1], -2)]
    for k in (1, 7, 2, 6, 3, 5):
        own[k] = over_z(own[k], k)
    opposite = [over_z(opposite[0], 2), over_z(opposite[1], -2)]
    recv = over_x(send)
    ring_k, ring_r = [keep] + [None] * (n_z - 1), [recv] + [None] * (n_z - 1)
    own[1], own[7], own[2], own[6], own[3], own[5], opposite[0], opposite[1], ring_k[0], ring_r[0] = tie(
        (own[1], own[7], own[2], own[6], own[3], own[5], opposite[0], opposite[1], ring_k[0], ring_r[0])
    )
    own_all = packed(own[:4] + opposite + own[5:])
    other_all = over_x(own_all)
    ring_k[1], ring_k[7] = over_z(ring_k[0], 1), over_z(ring_k[0], -1)
    ring_r[1], ring_r[7] = over_z(ring_r[0], 1), over_z(ring_r[0], -1)
    ring_k[1], ring_k[7] = tie((ring_k[1], ring_k[7]))
    ring_r[1], ring_r[7] = tie((ring_r[1], ring_r[7]))
    ring_k[2], ring_k[6] = over_z(ring_k[1], 1), over_z(ring_k[7], -1)
    ring_r[2], ring_r[6] = over_z(ring_r[1], 1), over_z(ring_r[7], -1)
    ring_k[2], ring_k[6] = tie((ring_k[2], ring_k[6]))
    ring_r[2], ring_r[6] = tie((ring_r[2], ring_r[6]))
    ring_k[3], ring_k[5] = over_z(ring_k[2], 1), over_z(ring_k[6], -1)
    ring_r[3], ring_r[5] = over_z(ring_r[2], 1), over_z(ring_r[6], -1)
    ring_k[3], ring_k[5] = tie((ring_k[3], ring_k[5]))
    ring_r[3], ring_r[5], other_all = tie((ring_r[3], ring_r[5], other_all))
    ring_k[4], ring_r[4] = over_z(ring_k[3], 1), over_z(ring_r[5], -1)

    a_sorted, product = pl.pallas_call(
        functools.partial(contract_most, n_z),
        out_shape=[
            jax.ShapeDtypeStruct((groups, *slab_shape.shape), jnp.bfloat16),
            jax.ShapeDtypeStruct((bands // STEP, STEP * n_state, half_columns), jnp.float32),
        ],
        in_specs=[VMEM] * (2 * n_z),
        out_specs=[VMEM] * 2,
        scratch_shapes=[pltpu.VMEM((2 * half_columns, half_columns), jnp.bfloat16)],
        compiler_params=limit,
    )(*in_vmem([own_all, other_all] + ring_k[:4] + ring_k[5:] + ring_r[:4] + ring_r[5:]))
    shares = pl.pallas_call(
        functools.partial(contract_rest, n_z),
        out_shape=jax.ShapeDtypeStruct((groups, n_state // groups, n_state), jnp.float32),
        in_specs=[SMEM] + [VMEM] * 4,
        out_specs=VMEM,
        scratch_shapes=[pltpu.VMEM((half_columns // 2, half_columns), jnp.bfloat16)],
        compiler_params=limit,
    )(weights, *in_vmem([a_sorted, product, ring_k[4], ring_r[4]]))

    layers = [[2 * z_at + x_at for x_at in range(2)] for z_at in range(n_z)]
    by_z = [[2 * z_at + x_at for z_at in range(n_z)] for x_at in range(2)]
    shares = shares.reshape(n_z, 2, *shares.shape[1:])
    share = jnp.sum(lax.all_to_all(shares, "ga", 0, 0, axis_index_groups=by_z, tiled=True), axis=0)
    n_pb = lax.axis_size("pb")
    copies = jnp.broadcast_to(share[None], (n_pb, *share.shape)).reshape(n_pb * 2, *share.shape[1:])
    planes = [[p * groups + i for p in range(n_pb) for i in layer] for layer in layers]
    received = lax.all_to_all(copies, ("pb", "ga"), 0, 0, axis_index_groups=planes, tiled=True)
    return jnp.sum(received, axis=0)


def solution(mesh):
    return jax.shard_map(
        on_device,
        mesh=mesh,
        in_specs=(P("pb", None, None, "ga"), P("pb", "ga", None), P("pb"), P("pb"), P()),
        out_specs=P("ga", None),
        check_vma=False,
    )
```
